32 devices in a mesh: row: 8 (over z, x), col: 4 (over y, core).
Axes of the slice: x: 2, y: 2, z: 4, core: 2. Of those that a mesh axis runs over, the one named last changes fastest.
Arguments:
- vectors: bfloat16 [4, 4, 8, 16, 256], P(None, 'col', 'row'), may hold values from -6 to 6
- tiles: bfloat16 [8, 4, 64, 256, 256], P('row', 'col'), may hold values from -0.0625 to 0.0625
- tile_coords: int32 [8, 4, 64, 2], P('row', 'col'), may hold values from 0 to 127, as said below
- tile_count: int32 [8, 4], P('row', 'col'), may hold values from 16 to 64, as said below
Outputs:
- product: float32 [4, 4, 8, 16, 256], P(None, 'col', 'row')
The draws below stay inside these ranges and needn't reach their ends.
Inputs may be any that keep to these rules, and one draw needn't show every extreme that they name: `tile_coords`: for the device in grid row r and grid column c every slot's block row I has I % 8 == r, its block column J has (J // 8) % 4 == c, and J <= I. `tile_count`: counts differ from device to device; in every draw some device uses all 64 slots and some other uses 64 // 4.
All inputs are finite; a program needn't handle non-finite values.
Results may differ from the reference program's by a relative error of at most 0.0003.
Values may be sent and summed in bfloat16 or wider, within the bound.
No kernel may reach another device: no remote copies, remote signals or barrier semaphores. Data moves between devices by JAX's collectives and lax.ppermute only.
A program may use at most 64 MiB of HBM per device.

```python
import jax
import jax.numpy as jnp
from jax import lax

NV = 16
B = 256
K = 4
TILES_DEV = 64
PR = 8
PC = 4
NBLK = 128


def draw_tile_coords(key, part):
    cells = PR * PC
    full_shape = (PR, PC, TILES_DEV)
    grid_row = jnp.arange(PR, dtype=jnp.int32)[:, None, None]
    grid_col = jnp.arange(PC, dtype=jnp.int32)[None, :, None]
    first_key, second_key = jax.random.split(key)
    lowest = jnp.broadcast_to(grid_col, full_shape)
    within_row = jax.random.randint(first_key, full_shape, lowest, K * PC)
    row_block = within_row // PC * cells + within_row % PC * PR + grid_row
    allowed = row_block // cells * PR + jnp.clip(row_block % cells - grid_col * PR + 1, 0, PR)
    within_col = jax.random.randint(second_key, full_shape, jnp.zeros(full_shape, jnp.int32), allowed)
    col_block = within_col // PR * cells + grid_col * PR + within_col % PR
    return jnp.stack([row_block, col_block], axis=-1).astype(jnp.int32)


def draw_tile_count(key, part):
    devices_all = PR * PC
    keys = jax.random.split(jax.random.fold_in(key, 7), 3)
    counts = jax.random.randint(keys[0], (devices_all,), TILES_DEV // 4, TILES_DEV + 1)
    fullest = jax.random.randint(keys[1], (), 0, devices_all)
    emptiest = (fullest + jax.random.randint(keys[2], (), 1, devices_all)) % devices_all
    device_ids = jnp.arange(devices_all, dtype=jnp.int32)
    counts = jnp.where(device_ids == fullest, TILES_DEV, counts)
    counts = jnp.where(device_ids == emptiest, TILES_DEV // 4, counts)
    return counts.reshape(PR, PC).astype(jnp.int32)


def steps_of(rng, extent, cuts, least, largest):
    gain = 1.0
    for position, shards_of in cuts:
        draws = jax.random.uniform(jax.random.fold_in(jax.random.fold_in(rng, 6), position), (shards_of,), jnp.float32, least / len(cuts), largest / len(cuts))
        gain = gain * jnp.repeat(jnp.exp(draws), extent[position] // shards_of).reshape((-1,) + (1,) * (len(extent) - 1 - position))
    return gain


def noise(rng, extent, scale, limit, shards=(), kind=jnp.bfloat16):
    loudness = steps_of(rng, extent, shards, -0.22, 0.18) if shards else 1.0
    result = jax.random.normal(rng, extent, jnp.float32) * scale * loudness
    return jnp.minimum(jnp.maximum(result, -limit), limit).astype(kind)


def setup_inputs(seed: int = 0) -> dict:
    streams_of = jax.random.split(jax.random.key(seed), 5)
    vectors = noise(streams_of[0], (K, PC, PR, NV, B), 1.0, 6.0, ((1, 4), (2, 8)))
    tiles = noise(streams_of[1], (PR, PC, TILES_DEV, B, B), (2 * B * TILES_DEV // K) ** -0.5, 0.0625, ((0, 8), (1, 4)))
    tile_coords = draw_tile_coords(jax.random.fold_in(streams_of[4], 71), 0)
    tile_count = draw_tile_count(jax.random.fold_in(streams_of[4], 71), 0)
    return {"vectors": vectors, "tiles": tiles, "tile_coords": tile_coords, "tile_count": tile_count}


def reference(vectors, tiles, tile_coords, tile_count):
    blocks = vectors.reshape(NBLK, NV, B).astype(jnp.float32)
    tile_sets = tiles.reshape(PR * PC, TILES_DEV, B, B)
    coord_sets = tile_coords.reshape(PR * PC, TILES_DEV, 2)
    filled_sets = tile_count.reshape(PR * PC)
    slot_ids = jnp.arange(TILES_DEV, dtype=jnp.int32)

    def device_step(total, device_item):
        matrices, positions, filled = device_item
        active = (slot_ids < filled).astype(jnp.float32)[:, None, None]
        row_block = positions[:, 0].astype(jnp.int32)
        col_block = positions[:, 1].astype(jnp.int32)
        dense = matrices.astype(jnp.float32)
        forward_part = jnp.einsum("snb,smb->snm", blocks[col_block], dense, precision=lax.Precision.HIGHEST) * active
        mirror_part = jnp.einsum("snb,sbm->snm", blocks[row_block], dense, precision=lax.Precision.HIGHEST) * active
        total = total.at[row_block].add(forward_part)
        total = total.at[col_block].add(mirror_part)
        return total, None

    start_total = jnp.zeros((NBLK, NV, B), jnp.float32)
    total, _ = lax.scan(device_step, start_total, (tile_sets, coord_sets, filled_sets))
    return total.reshape(K, PC, PR, NV, B)
```

```python
import functools

import jax
import jax.numpy as jnp
from jax import lax
from jax.experimental import pallas as pl
from jax.experimental.pallas import tpu as pltpu
from jax.sharding import PartitionSpec as P

GROUP = 16
LEVELS = 32000.0
TINY = 1e-30
ROWS_MIN = 8


def extra_rows(repeats):
    return -(-repeats // ROWS_MIN) * ROWS_MIN


def encode(blocks, out):
    repeats = len(blocks)
    vec, width = blocks[0].shape
    tail = extra_rows(repeats)
    row = lax.broadcasted_iota(jnp.int32, (tail, width), 0)
    exponents = jnp.zeros((tail, width), jnp.float32)
    for k, block in enumerate(blocks):
        top = jnp.max(jnp.abs(block), axis=0, keepdims=True)
        exponent = jnp.ceil(jnp.log2(jnp.maximum(top, TINY)))
        coded = block * jnp.exp2(-exponent) * LEVELS
        out[k * vec : (k + 1) * vec, :] = jnp.round(coded).astype(jnp.int32).astype(jnp.int16)
        exponents = jnp.where(row == k, exponent, exponents)
    out[repeats * vec :, :] = exponents.astype(jnp.int32).astype(jnp.int16)


def decode(coded, repeats, vec):
    tail = coded[repeats * vec :, :].astype(jnp.int32).astype(jnp.float32)
    scales = jnp.exp2(tail) * (1.0 / LEVELS)
    return [
        coded[k * vec : (k + 1) * vec, :].astype(jnp.int32).astype(jnp.float32) * scales[k : k + 1, :]
        for k in range(repeats)
    ]


def places(coords, s, rows, cols, repeats):
    upper, lower = coords[s, 0], coords[s, 1]
    cells = rows * cols
    own_row = lax.rem(upper, rows)
    own_col = lax.rem(lax.div(lower, rows), cols)
    upper_col = lax.div(lax.rem(upper, cells), rows)
    lower_row = lax.rem(lower, rows)
    upper_at = (upper_col ^ own_col) * repeats + lax.div(upper, cells)
    lower_owner = lower_row * repeats + lax.div(lower, cells)
    lower_at = (lower_row ^ own_row) * repeats + lax.div(lower, cells)
    return upper_at, lower_owner, lower_at


def load_pieces(pieces, held, repeats):
    at = 0
    for piece in pieces:
        count = piece.shape[0]
        held[at : at + count] = piece[...]
        at += count


def mirror_kernel(rows, cols, repeats, count, coords, tiles, *refs):
    *pieces, out, held, total = refs
    load_pieces(pieces, held, repeats)
    total[...] = jnp.zeros_like(total)
    filled = count[0, 0]

    def turn(g, carry):
        for q in range(GROUP):
            s = g * GROUP + q
            upper_at, lower_owner, _ = places(coords, s, rows, cols, repeats)
            x = held[upper_at]
            x = jnp.where(s < filled, x, jnp.zeros_like(x))
            total[lower_owner] += jnp.dot(x, tiles[s], preferred_element_type=jnp.float32)
        return carry

    lax.fori_loop(0, lax.div(filled + GROUP - 1, GROUP), turn, 0)

    def chunk(p, carry):
        encode([total[p * repeats + k] for k in range(repeats)], out.at[p])
        return carry

    lax.fori_loop(0, rows, chunk, 0)


def forward_kernel(rows, cols, repeats, count, coords, tiles, *refs):
    pieces, outs, held, total = refs[: -cols - 2], refs[-cols - 2 : -2], refs[-2], refs[-1]
    load_pieces(pieces, held, repeats)
    total[...] = jnp.zeros_like(total)
    filled = count[0, 0]

    def turn(g, carry):
        for q in range(GROUP):
            s = g * GROUP + q
            upper_at, _, lower_at = places(coords, s, rows, cols, repeats)
            x = held[lower_at]
            x = jnp.where(s < filled, x, jnp.zeros_like(x))
            total[upper_at] += lax.dot_general(
                x, tiles[s], (((1,), (1,)), ((), ())), preferred_element_type=jnp.float32
            )
        return carry

    lax.fori_loop(0, lax.div(filled + GROUP - 1, GROUP), turn, 0)
    outs[0][...] = total[0:repeats]
    for o in range(1, cols):
        encode([total[o * repeats + k] for k in range(repeats)], outs[o])


def final_kernel(rows, repeats, mirrored, own, *refs):
    *received, out = refs
    vec = own.shape[1]
    sums = [own[k] for k in range(repeats)]
    for ref in [mirrored.at[p] for p in range(rows)] + received:
        sums = [a + b for a, b in zip(sums, decode(ref, repeats, vec))]
    for k in range(repeats):
        out[k] = sums[k]


def partners(n, offset):
    return [(i, i ^ offset) for i in range(n)]


def body(vectors, tiles, tile_coords, tile_count):
    rows, cols = lax.axis_size("row"), lax.axis_size("col")
    repeats, vec, width = vectors.shape[0], vectors.shape[3], vectors.shape[4]
    slots = tiles.shape[2]
    if rows & (rows - 1) or cols & (cols - 1) or slots % GROUP:
        raise ValueError("sizes")
    mine = vectors.reshape(repeats, vec, width)
    mats = tiles.reshape(slots, width, width)
    coords = tile_coords.reshape(slots, 2)
    coded_rows = repeats * vec + extra_rows(repeats)

    pieces, offsets = [mine], [0]
    bit = cols // 2
    while bit:
        pieces += [lax.ppermute(piece, "col", partners(cols, bit)) for piece in pieces]
        offsets += [o ^ bit for o in offsets]
        bit //= 2
    row_pieces = [piece for _, piece in sorted(zip(offsets, pieces), key=lambda pair: pair[0])]

    held = mine[None]
    bit = rows // 2
    while bit:
        other = lax.ppermute(held, "row", partners(rows, bit))
        held = jnp.stack([held, other], axis=1).reshape(-1, repeats, vec, width)
        bit //= 2
    column_blocks = held.reshape(rows * repeats, vec, width)

    smem = pl.BlockSpec(memory_space=pltpu.SMEM)
    vmem = pl.BlockSpec(memory_space=pltpu.VMEM)
    params = pltpu.CompilerParams(vmem_limit_bytes=24 << 20)
    cost = pl.CostEstimate(
        flops=2 * slots * vec * width * width, bytes_accessed=2 * slots * width * width, transcendentals=0
    )
    mirrored = pl.pallas_call(
        functools.partial(mirror_kernel, rows, cols, repeats),
        out_shape=jax.ShapeDtypeStruct((rows, coded_rows, width), jnp.int16),
        in_specs=[smem, smem] + [vmem] * (1 + cols),
        out_specs=vmem,
        scratch_shapes=[
            pltpu.VMEM((cols * repeats, vec, width), jnp.bfloat16),
            pltpu.VMEM((rows * repeats, vec, width), jnp.float32),
        ],
        compiler_params=params,
        cost_estimate=cost,
        name="mirror",
    )(tile_count, coords, mats, *row_pieces)
    mirrored = lax.all_to_all(mirrored, "row", 0, 0, tiled=True)

    coded = jax.ShapeDtypeStruct((coded_rows, width), jnp.int16)
    own, *partial = pl.pallas_call(
        functools.partial(forward_kernel, rows, cols, repeats),
        out_shape=[jax.ShapeDtypeStruct((repeats, vec, width), jnp.float32)] + [coded] * (cols - 1),
        in_specs=[smem, smem] + [vmem] * 2,
        out_specs=[vmem] * cols,
        scratch_shapes=[
            pltpu.VMEM((rows * repeats, vec, width), jnp.bfloat16),
            pltpu.VMEM((cols * repeats, vec, width), jnp.float32),
        ],
        compiler_params=params,
        cost_estimate=cost,
        name="forward",
    )(tile_count, coords, mats, column_blocks)
    received = [lax.ppermute(part, "col", partners(cols, o + 1)) for o, part in enumerate(partial)]

    out = pl.pallas_call(
        functools.partial(final_kernel, rows, repeats),
        out_shape=jax.ShapeDtypeStruct((repeats, vec, width), jnp.float32),
        in_specs=[vmem] * (1 + cols),
        out_specs=vmem,
        compiler_params=params,
        name="final",
    )(mirrored, own, *received)
    return out.reshape(repeats, 1, 1, vec, width)


def solution(mesh):
    return jax.shard_map(
        body,
        mesh=mesh,
        in_specs=(
            P(None, "col", "row", None, None),
            P("row", "col", None, None, None),
            P("row", "col", None, None),
            P("row", "col"),
        ),
        out_specs=P(None, "col", "row", None, None),
        check_vma=False,
    )
```

```python
import functools

import jax
import jax.numpy as jnp
from jax import lax
from jax.experimental import pallas as pl
from jax.experimental.pallas import tpu as pltpu
from jax.sharding import PartitionSpec as P


GROUP = 8
LEVELS = 32000.0
TINY = 1e-30
ROWS_MIN = 8


def extra_rows(repeats):
    return -(-repeats // ROWS_MIN) * ROWS_MIN


def encode(blocks, out):
    repeats = len(blocks)
    vec, width = blocks[0].shape
    tail = extra_rows(repeats)
    row = lax.broadcasted_iota(jnp.int32, (tail, width), 0)
    exponents = jnp.zeros((tail, width), jnp.float32)
    for k, block in enumerate(blocks):
        top = jnp.max(jnp.abs(block), axis=0, keepdims=True)
        exponent = jnp.ceil(jnp.log2(jnp.maximum(top, TINY)))
        coded = block * jnp.exp2(-exponent) * LEVELS
        out[k * vec : (k + 1) * vec, :] = jnp.round(coded).astype(jnp.int32).astype(jnp.int16)
        exponents = jnp.where(row == k, exponent, exponents)
    out[repeats * vec :, :] = exponents.astype(jnp.int32).astype(jnp.int16)


def decode(coded, repeats, vec):
    tail = coded[repeats * vec :, :].astype(jnp.int32).astype(jnp.float32)
    scales = jnp.exp2(tail) * (1.0 / LEVELS)
    return [
        coded[k * vec : (k + 1) * vec, :].astype(jnp.int32).astype(jnp.float32) * scales[k : k + 1, :]
        for k in range(repeats)
    ]


def mirrored_bits(value, n):
    bits = n.bit_length() - 1
    turned = 0
    for i in range(bits):
        turned += ((value >> i) & 1) << (bits - 1 - i)
    return turned


def places(coords, s, rows, cols, repeats):
    upper, lower = coords[0, s], coords[1, s]
    cells = rows * cols
    own_row = lax.rem(upper, rows)
    own_col = lax.rem(lax.div(lower, rows), cols)
    upper_col = lax.div(lax.rem(upper, cells), rows)
    lower_row = lax.rem(lower, rows)
    upper_at = (upper_col ^ own_col) * repeats + lax.div(upper, cells)
    lower_owner = lower_row * repeats + lax.div(lower, cells)
    lower_at = mirrored_bits(lower_row ^ own_row, rows) * repeats + lax.div(lower, cells)
    return upper_at, lower_owner, lower_at


def load_pieces(pieces, held):
    at = 0
    for piece in pieces:
        count = piece.shape[0]
        held[at : at + count] = piece[...]
        at += count


def stream(tiles, stage, arrived, turns):
    def fetch(g):
        part = pl.ds(g * GROUP, GROUP)
        return pltpu.make_async_copy(tiles.at[part], stage.at[part], arrived.at[g])

    for g in range(tiles.shape[0] // GROUP):

        @pl.when(g < turns)
        def _():
            fetch(g).start()

    return fetch


def mirror_kernel(rows, cols, repeats, count, coords_far, tiles, *refs):
    *pieces, out, held, total, coded, coords, stage, arrived, listed, sent = refs
    filled = count[0, 0]
    turns = lax.div(filled + GROUP - 1, GROUP)
    listing = pltpu.make_async_copy(coords_far, coords, listed)
    listing.start()
    fetch = stream(tiles, stage, arrived, turns)
    load_pieces(pieces, held)
    total[...] = jnp.zeros_like(total)
    listing.wait()

    def turn(g, carry):
        fetch(g).wait()
        for q in range(GROUP):
            s = g * GROUP + q
            upper_at, lower_owner, _ = places(coords, s, rows, cols, repeats)
            x = held[upper_at]
            x = jnp.where(s < filled, x, jnp.zeros_like(x))
            total[lower_owner] += jnp.dot(x, stage[s], preferred_element_type=jnp.float32)
        return carry

    lax.fori_loop(0, turns, turn, 0)

    def send(p):
        return pltpu.make_async_copy(coded.at[p], out.at[p], sent.at[p])

    def chunk(p, carry):
        encode([total[p * repeats + k] for k in range(repeats)], coded.at[p])
        send(p).start()
        return carry

    lax.fori_loop(0, rows, chunk, 0)
    for p in range(rows):
        send(p).wait()


def forward_kernel(rows, cols, repeats, count, coords_far, tiles, *refs):
    *refs, held, total, coords, stage, arrived, listed = refs
    pieces, outs = refs[:-cols], refs[-cols:]
    filled = count[0, 0]
    turns = lax.div(filled + GROUP - 1, GROUP)
    listing = pltpu.make_async_copy(coords_far, coords, listed)
    listing.start()
    fetch = stream(tiles, stage, arrived, turns)
    load_pieces(pieces, held)
    total[...] = jnp.zeros_like(total)
    listing.wait()

    def turn(g, carry):
        fetch(g).wait()
        for q in range(GROUP):
            s = g * GROUP + q
            upper_at, _, lower_at = places(coords, s, rows, cols, repeats)
            x = held[lower_at]
            x = jnp.where(s < filled, x, jnp.zeros_like(x))
            total[upper_at] += lax.dot_general(
                x, stage[s], (((1,), (1,)), ((), ())), preferred_element_type=jnp.float32
            )
        return carry

    lax.fori_loop(0, turns, turn, 0)
    outs[0][...] = total[0:repeats]
    for o in range(1, cols):
        encode([total[o * repeats + k] for k in range(repeats)], outs[o])


def final_kernel(rows, repeats, mirrored, own, *refs):
    *received, out = refs
    vec = own.shape[1]
    sums = [own[k] for k in range(repeats)]
    for ref in [mirrored.at[p] for p in range(rows)] + received:
        sums = [a + b for a, b in zip(sums, decode(ref, repeats, vec))]
    for k in range(repeats):
        out[k] = sums[k]


def prepare_kernel(vectors, out):
    out[...] = vectors[...]


def partners(n, offset):
    return [(i, i ^ offset) for i in range(n)]


def body(vectors, tiles, tile_coords, tile_count):
    rows, cols = lax.axis_size("row"), lax.axis_size("col")
    repeats, vec, width = vectors.shape[0], vectors.shape[3], vectors.shape[4]
    slots = tiles.shape[2]
    if rows & (rows - 1) or cols & (cols - 1) or slots % GROUP:
        raise ValueError("sizes")
    mine = vectors.reshape(repeats, vec, width)
    mats = tiles.reshape(slots, width, width)
    coords = tile_coords.reshape(slots, 2).T
    coded_rows = repeats * vec + extra_rows(repeats)

    vmem = pl.BlockSpec(memory_space=pltpu.VMEM)
    near = pl.pallas_call(
        prepare_kernel,
        out_shape=jax.ShapeDtypeStruct(mine.shape, mine.dtype),
        in_specs=[vmem],
        out_specs=vmem,
        compiler_params=pltpu.CompilerParams(vmem_limit_bytes=2 << 20),
        cost_estimate=pl.CostEstimate(flops=0, bytes_accessed=2 * slots * width * width, transcendentals=0),
        name="prepare",
    )(mine)

    pieces, offsets = [mine], [0]
    bit = cols // 2
    while bit:
        moved = []
        for piece in pieces:
            moved.append(lax.ppermute(piece, "col", partners(cols, bit)))
        pieces += moved
        offsets += [o ^ bit for o in offsets]
        bit //= 2
    pieces[0] = near
    row_pieces = [piece for _, piece in sorted(zip(offsets, pieces), key=lambda pair: pair[0])]

    column_pieces = [near]
    bit = rows // 2
    while bit:
        held = jnp.concatenate(column_pieces, axis=0) if bit < rows // 2 else mine
        column_pieces.append(lax.ppermute(held, "row", partners(rows, bit)))
        bit //= 2

    smem = pl.BlockSpec(memory_space=pltpu.SMEM)
    params = pltpu.CompilerParams(vmem_limit_bytes=60 << 20)
    cost = pl.CostEstimate(
        flops=2 * slots * vec * width * width, bytes_accessed=2 * slots * width * width, transcendentals=0
    )
    far = pl.BlockSpec(memory_space=pl.ANY)
    mirrored = pl.pallas_call(
        functools.partial(mirror_kernel, rows, cols, repeats),
        out_shape=jax.ShapeDtypeStruct((rows, coded_rows, width), jnp.int16),
        in_specs=[smem, far, far] + [vmem] * cols,
        out_specs=far,
        scratch_shapes=[
            pltpu.VMEM((cols * repeats, vec, width), jnp.bfloat16),
            pltpu.VMEM((rows * repeats, vec, width), jnp.float32),
            pltpu.VMEM((rows, coded_rows, width), jnp.int16),
            pltpu.SMEM(coords.shape, coords.dtype),
            pltpu.VMEM(mats.shape, mats.dtype),
            pltpu.SemaphoreType.DMA((slots // GROUP,)),
            pltpu.SemaphoreType.DMA,
            pltpu.SemaphoreType.DMA((rows,)),
        ],
        compiler_params=params,
        cost_estimate=cost,
        name="mirror",
    )(tile_count, coords, mats, *row_pieces)
    mirrored = lax.all_to_all(mirrored, "row", 0, 0, tiled=True)

    coded = jax.ShapeDtypeStruct((coded_rows, width), jnp.int16)
    own, *partial = pl.pallas_call(
        functools.partial(forward_kernel, rows, cols, repeats),
        out_shape=[jax.ShapeDtypeStruct((repeats, vec, width), jnp.float32)] + [coded] * (cols - 1),
        in_specs=[smem, far, far] + [vmem] * len(column_pieces),
        out_specs=[vmem] * cols,
        scratch_shapes=[
            pltpu.VMEM((rows * repeats, vec, width), jnp.bfloat16),
            pltpu.VMEM((cols * repeats, vec, width), jnp.float32),
            pltpu.SMEM(coords.shape, coords.dtype),
            pltpu.VMEM(mats.shape, mats.dtype),
            pltpu.SemaphoreType.DMA((slots // GROUP,)),
            pltpu.SemaphoreType.DMA,
        ],
        compiler_params=params,
        cost_estimate=cost,
        name="forward",
    )(tile_count, coords, mats, *column_pieces)
    received = [lax.ppermute(part, "col", partners(cols, o + 1)) for o, part in enumerate(partial)]

    out = pl.pallas_call(
        functools.partial(final_kernel, rows, repeats),
        out_shape=jax.ShapeDtypeStruct((repeats, vec, width), jnp.float32),
        in_specs=[vmem] * (1 + cols),
        out_specs=vmem,
        compiler_params=pltpu.CompilerParams(vmem_limit_bytes=8 << 20),
        name="final",
    )(mirrored, own, *received)
    return out.reshape(repeats, 1, 1, vec, width)


def solution(mesh):
    return jax.shard_map(
        body,
        mesh=mesh,
        in_specs=(
            P(None, "col", "row", None, None),
            P("row", "col", None, None, None),
            P("row", "col", None, None),
            P("row", "col"),
        ),
        out_specs=P(None, "col", "row", None, None),
        check_vma=False,
    )
```

```python
import functools

import jax
import jax.numpy as jnp
from jax import lax
from jax.experimental import pallas as pl
from jax.experimental.pallas import tpu as pltpu
from jax.sharding import PartitionSpec as P


GROUP = 16
LEVELS = 32000.0
TINY = 1e-30
ROWS_MIN = 8


def extra_rows(repeats):
    return -(-repeats // ROWS_MIN) * ROWS_MIN


def encode(blocks, out):
    repeats = len(blocks)
    vec, width = blocks[0].shape
    tail = extra_rows(repeats)
    row = lax.broadcasted_iota(jnp.int32, (tail, width), 0)
    exponents = jnp.zeros((tail, width), jnp.float32)
    for k, block in enumerate(blocks):
        top = jnp.max(jnp.abs(block), axis=0, keepdims=True)
        exponent = jnp.ceil(jnp.log2(jnp.maximum(top, TINY)))
        coded = block * jnp.exp2(-exponent) * LEVELS
        out[k * vec : (k + 1) * vec, :] = jnp.round(coded).astype(jnp.int32).astype(jnp.int16)
        exponents = jnp.where(row == k, exponent, exponents)
    out[repeats * vec :, :] = exponents.astype(jnp.int32).astype(jnp.int16)


def decode(coded, repeats, vec):
    tail = coded[repeats * vec :, :].astype(jnp.int32).astype(jnp.float32)
    scales = jnp.exp2(tail) * (1.0 / LEVELS)
    return [
        coded[k * vec : (k + 1) * vec, :].astype(jnp.int32).astype(jnp.float32) * scales[k : k + 1, :]
        for k in range(repeats)
    ]


def mirrored_bits(value, n):
    bits = n.bit_length() - 1
    turned = 0
    for i in range(bits):
        turned += ((value >> i) & 1) << (bits - 1 - i)
    return turned


def places(coords, s, rows, cols, repeats):
    upper, lower = coords[0, s], coords[1, s]
    cells = rows * cols
    own_row = lax.rem(upper, rows)
    own_col = lax.rem(lax.div(lower, rows), cols)
    upper_col = lax.div(lax.rem(upper, cells), rows)
    away = lax.rem(lower, rows) ^ own_row
    upper_at = (upper_col ^ own_col) * repeats + lax.div(upper, cells)
    lower_out = away * repeats + lax.div(lower, cells)
    lower_at = mirrored_bits(away, rows) * repeats + lax.div(lower, cells)
    return upper_at, lower_out, lower_at


def multiply(count, tiles, held, total, at, contracted):
    filled = count[0]
    total[...] = jnp.zeros_like(total)

    def turn(g, carry):
        for q in range(GROUP):
            s = g * GROUP + q
            source, target = at(s)
            x = held[source]
            x = jnp.where(s < filled, x, jnp.zeros_like(x))
            total[target] += lax.dot_general(
                x, tiles[s], (((1,), (contracted,)), ((), ())), preferred_element_type=jnp.float32
            )
        return carry

    lax.fori_loop(0, lax.div(filled + GROUP - 1, GROUP), turn, 0)


def load_pieces(pieces, held):
    at = 0
    for piece in pieces:
        count = piece.shape[0]
        held[at : at + count] = piece[...]
        at += count


def mirror_kernel(rows, cols, repeats, away, count, coords, tiles, *refs):
    *pieces, total, coded, held = refs
    load_pieces(pieces, held)

    def at(s):
        upper_at, lower_out, _ = places(coords, s, rows, cols, repeats)
        return upper_at, lower_out

    multiply(count, tiles, held, total, at, 0)
    for i, o in enumerate(away):
        encode([total[o * repeats + k] for k in range(repeats)], coded.at[i])


def forward_kernel(rows, cols, repeats, count, coords, tiles, *refs):
    *refs, held, total = refs
    pieces, outs = refs[:-cols], refs[-cols:]
    load_pieces(pieces, held)

    def at(s):
        upper_at, _, lower_at = places(coords, s, rows, cols, repeats)
        return lower_at, upper_at

    multiply(count, tiles, held, total, at, 1)
    outs[0][...] = total[0:repeats]
    for o in range(1, cols):
        encode([total[o * repeats + k] for k in range(repeats)], outs[o])


def fold_kernel(repeats, vec, kept, away, total, received, *outs):
    kept_out, coded = outs
    for i, o in enumerate(kept):
        sums = decode(received.at[i], repeats, vec)
        sums = [total[o * repeats + k] + sums[k] for k in range(repeats)]
        if i in away:
            encode(sums, coded.at[away.index(i)])
        else:
            at = [j for j in range(len(kept)) if j not in away].index(i)
            for k in range(repeats):
                kept_out[at * repeats + k] = sums[k]


def final_kernel(repeats, own_rows, own_cols, *refs):
    *received, out = refs
    vec = own_rows.shape[1]
    sums = [own_rows[k] + own_cols[k] for k in range(repeats)]
    for ref in received:
        sums = [a + b for a, b in zip(sums, decode(ref, repeats, vec))]
    for k in range(repeats):
        out[k] = sums[k]


def anchor_kernel(out):
    out[...] = jnp.zeros_like(out)


def prepare_kernel(anchor, vectors_far, vectors, arrived):
    copy = pltpu.make_async_copy(vectors_far, vectors, arrived)
    copy.start()
    copy.wait()


def halving(n):
    bits = [1 << i for i in reversed(range(n.bit_length() - 1))]
    return bits[1:] + bits[:1]


def partners(n, offset):
    return [(i, i ^ offset) for i in range(n)]


def body(vectors, tiles, tile_coords, tile_count):
    rows, cols = lax.axis_size("row"), lax.axis_size("col")
    repeats, vec, width = vectors.shape[0], vectors.shape[3], vectors.shape[4]
    slots = tiles.shape[2]
    if rows & (rows - 1) or cols & (cols - 1) or slots % GROUP:
        raise ValueError("sizes")
    mine = vectors.reshape(repeats, vec, width)
    mats = tiles.reshape(slots, width, width)
    coords = tile_coords.reshape(slots, 2).T
    coded_rows = repeats * vec + extra_rows(repeats)

    vmem = pl.BlockSpec(memory_space=pltpu.VMEM)
    far = pl.BlockSpec(memory_space=pl.ANY)
    anchor = pl.pallas_call(
        anchor_kernel,
        out_shape=jax.ShapeDtypeStruct((8, 128), jnp.float32),
        out_specs=vmem,
        compiler_params=pltpu.CompilerParams(vmem_limit_bytes=1 << 20),
        cost_estimate=pl.CostEstimate(flops=1 << 36, bytes_accessed=1 << 10, transcendentals=0),
        name="anchor",
    )()
    near = pl.pallas_call(
        prepare_kernel,
        out_shape=jax.ShapeDtypeStruct(mine.shape, mine.dtype),
        in_specs=[vmem, far],
        out_specs=vmem,
        scratch_shapes=[pltpu.SemaphoreType.DMA],
        compiler_params=pltpu.CompilerParams(vmem_limit_bytes=2 << 20),
        cost_estimate=pl.CostEstimate(flops=0, bytes_accessed=1 << 20, transcendentals=0),
        name="prepare",
    )(anchor, mine)
    filled = tile_count.reshape(1)

    pieces, offsets = [mine], [0]
    bit = cols // 2
    while bit:
        moved = []
        for piece in pieces:
            moved.append(lax.ppermute(piece, "col", partners(cols, bit)))
        pieces += moved
        offsets += [o ^ bit for o in offsets]
        bit //= 2
    pieces[0] = near
    row_pieces = [piece for _, piece in sorted(zip(offsets, pieces), key=lambda pair: pair[0])]

    column_pieces = [near]
    bit = rows // 2
    while bit:
        held = jnp.concatenate(column_pieces, axis=0) if bit < rows // 2 else mine
        column_pieces.append(lax.ppermute(held, "row", partners(rows, bit)))
        bit //= 2

    smem = pl.BlockSpec(memory_space=pltpu.SMEM)
    params = pltpu.CompilerParams(vmem_limit_bytes=16 << 20)
    cost = pl.CostEstimate(
        flops=2 * slots * vec * width * width, bytes_accessed=2 * slots * width * width, transcendentals=0
    )
    small = pl.CostEstimate(flops=0, bytes_accessed=1 << 20, transcendentals=0)

    def coded(n):
        return jax.ShapeDtypeStruct((n, coded_rows, width), jnp.int16)

    def blocks(n):
        return jax.ShapeDtypeStruct((n * repeats, vec, width), jnp.float32)

    order = halving(rows)
    held = list(range(rows))
    away = [o for o in held if o & order[0]]
    total, sent = pl.pallas_call(
        functools.partial(mirror_kernel, rows, cols, repeats, away),
        out_shape=[blocks(rows), coded(len(away))],
        in_specs=[smem, smem] + [vmem] * (1 + cols),
        out_specs=[vmem, vmem],
        scratch_shapes=[pltpu.VMEM((cols * repeats, vec, width), jnp.bfloat16)],
        compiler_params=params,
        cost_estimate=cost,
        name="mirror",
    )(filled, coords, mats, *row_pieces)
    for step, bit in enumerate(order):
        received = lax.ppermute(sent, "row", partners(rows, bit))
        if step == len(order) - 1:
            break
        stay = [i for i, o in enumerate(held) if not o & bit]
        left = [held[i] for i in stay]
        following = order[step + 1]
        go = [i for i, o in enumerate(left) if o & following]
        total, sent = pl.pallas_call(
            functools.partial(fold_kernel, repeats, vec, stay, go),
            out_shape=[blocks(len(left) - len(go)), coded(len(go))],
            in_specs=[vmem, vmem],
            out_specs=[vmem, vmem],
            compiler_params=params,
            cost_estimate=small,
        )(total, received)
        held = [o for o in left if not o & following]

    own, *partial = pl.pallas_call(
        functools.partial(forward_kernel, rows, cols, repeats),
        out_shape=[blocks(1)] + [jax.ShapeDtypeStruct((coded_rows, width), jnp.int16)] * (cols - 1),
        in_specs=[smem, smem] + [vmem] * (1 + len(column_pieces)),
        out_specs=[vmem] * cols,
        scratch_shapes=[
            pltpu.VMEM((rows * repeats, vec, width), jnp.bfloat16),
            pltpu.VMEM((cols * repeats, vec, width), jnp.float32),
        ],
        compiler_params=params,
        cost_estimate=cost,
        name="forward",
    )(filled, coords, mats, *column_pieces)
    gathered = []
    for o, part in enumerate(partial):
        gathered.append(lax.ppermute(part, "col", partners(cols, o + 1)))

    out = pl.pallas_call(
        functools.partial(final_kernel, repeats),
        out_shape=blocks(1),
        in_specs=[vmem] * (2 + cols),
        out_specs=vmem,
        compiler_params=params,
        name="final",
    )(total, own, received.reshape(coded_rows, width), *gathered)
    return out.reshape(repeats, 1, 1, vec, width)


def solution(mesh):
    return jax.shard_map(
        body,
        mesh=mesh,
        in_specs=(
            P(None, "col", "row", None, None),
            P("row", "col", None, None, None),
            P("row", "col", None, None),
            P("row", "col"),
        ),
        out_specs=P(None, "col", "row", None, None),
        check_vma=False,
    )
```

```python
import functools

import jax
import jax.numpy as jnp
from jax import lax
from jax.experimental import pallas as pl
from jax.experimental.pallas import tpu as pltpu
from jax.sharding import PartitionSpec as P


GROUP = 16
LEVELS = 32000.0
TINY = 1e-30
ROWS_MIN = 8


def extra_rows(repeats):
    return -(-repeats // ROWS_MIN) * ROWS_MIN


def encode(blocks, out):
    repeats = len(blocks)
    vec, width = blocks[0].shape
    tail = extra_rows(repeats)
    row = lax.broadcasted_iota(jnp.int32, (tail, width), 0)
    exponents = jnp.zeros((tail, width), jnp.float32)
    for k, block in enumerate(blocks):
        top = jnp.max(jnp.abs(block), axis=0, keepdims=True)
        exponent = jnp.ceil(jnp.log2(jnp.maximum(top, TINY)))
        coded = block * jnp.exp2(-exponent) * LEVELS
        out[k * vec : (k + 1) * vec, :] = jnp.round(coded).astype(jnp.int32).astype(jnp.int16)
        exponents = jnp.where(row == k, exponent, exponents)
    out[repeats * vec :, :] = exponents.astype(jnp.int32).astype(jnp.int16)


def decode(coded, repeats, vec):
    tail = coded[repeats * vec :, :].astype(jnp.int32).astype(jnp.float32)
    scales = jnp.exp2(tail) * (1.0 / LEVELS)
    return [
        coded[k * vec : (k + 1) * vec, :].astype(jnp.int32).astype(jnp.float32) * scales[k : k + 1, :]
        for k in range(repeats)
    ]


def mirrored_bits(value, n):
    bits = n.bit_length() - 1
    turned = 0
    for i in range(bits):
        turned += ((value >> i) & 1) << (bits - 1 - i)
    return turned


def log2(n):
    return n.bit_length() - 1


def gathering(n):
    return [1 << i for i in reversed(range(log2(n)))]


class Places:
    def __init__(self, coords, rows, cols, repeats):
        self.coords, self.rows, self.cols, self.repeats = coords, rows, cols, repeats
        self.cells = log2(rows * cols)

    def away(self, s):
        return (self.coords[0, s] ^ self.coords[1, s]) & (self.rows - 1)

    def row_block(self, s):
        upper, lower = self.coords[0, s], self.coords[1, s]
        across = ((upper >> log2(self.rows)) ^ (lower >> log2(self.rows))) & (self.cols - 1)
        return across * self.repeats + (upper >> self.cells)

    def column_block(self, s, place):
        return place * self.repeats + (self.coords[1, s] >> self.cells)


def multiply(start, stop, listed, tiles, held, total, at, contracted):
    slots = tiles.shape[0]

    def turn(g, carry):
        for q in range(GROUP):
            i = start + g * GROUP + q
            s = jnp.clip(listed(i), 0, slots - 1)
            source, target = at(s)
            x = held[source]
            x = jnp.where(i < stop, x, jnp.zeros_like(x))
            total[target] += lax.dot_general(
                x, tiles[s], (((1,), (contracted,)), ((), ())), preferred_element_type=jnp.float32
            )
        return carry

    lax.fori_loop(0, lax.div(stop - start + GROUP - 1, GROUP), turn, 0)


def load_pieces(pieces, held):
    at = 0
    for piece in pieces:
        count = piece.shape[0]
        held[at : at + count] = piece[...]
        at += count


def mirror_kernel(rows, cols, repeats, away, count, coords, tiles, *refs):
    *pieces, total, coded, held = refs
    load_pieces(pieces, held)
    places = Places(coords, rows, cols, repeats)
    total[...] = jnp.zeros_like(total)

    def at(s):
        return places.row_block(s), places.column_block(s, places.away(s))

    multiply(0, count[0], lambda i: i, tiles, held, total, at, 0)
    for i, o in enumerate(away):
        encode([total[o * repeats + k] for k in range(repeats)], coded.at[i])


def early_kernel(rows, cols, repeats, splits, lists, coords, tiles, *refs):
    *pieces, total, held = refs
    load_pieces(pieces, held)
    places = Places(coords, rows, cols, repeats)
    total[...] = jnp.zeros_like(total)

    def at(s):
        place = mirrored_bits(places.away(s), rows) & (rows // 2 - 1)
        return places.column_block(s, place), places.row_block(s)

    multiply(0, splits[0], lambda i: lists[i], tiles, held, total, at, 1)


def forward_kernel(rows, cols, repeats, splits, lists, coords, tiles, begun, held, *refs):
    *outs, total = refs
    places = Places(coords, rows, cols, repeats)
    total[...] = begun[...]

    def at(s):
        place = mirrored_bits(places.away(s), rows) & (rows // 2 - 1)
        return places.column_block(s, place), places.row_block(s)

    multiply(splits[1], tiles.shape[0], lambda i: lists[i], tiles, held, total, at, 1)
    outs[0][...] = total[0:repeats]
    for o in range(1, cols):
        encode([total[o * repeats + k] for k in range(repeats)], outs[o])


def fold_kernel(repeats, vec, kept, away, total, received, *outs):
    kept_out, coded = outs
    for i, o in enumerate(kept):
        sums = decode(received.at[i], repeats, vec)
        sums = [total[o * repeats + k] + sums[k] for k in range(repeats)]
        if i in away:
            encode(sums, coded.at[away.index(i)])
        else:
            at = [j for j in range(len(kept)) if j not in away].index(i)
            for k in range(repeats):
                kept_out[at * repeats + k] = sums[k]


def final_kernel(repeats, own_rows, own_cols, *refs):
    *received, out = refs
    vec = own_rows.shape[1]
    sums = [own_rows[k] + own_cols[k] for k in range(repeats)]
    for ref in received:
        sums = [a + b for a, b in zip(sums, decode(ref, repeats, vec))]
    for k in range(repeats):
        out[k] = sums[k]


def anchor_kernel(out):
    out[...] = jnp.zeros_like(out)


def prepare_kernel(anchor, vectors_far, vectors, arrived):
    copy = pltpu.make_async_copy(vectors_far, vectors, arrived)
    copy.start()
    copy.wait()


def plan_kernel(rows, slots, count, coords, after, splits, lists):
    late = log2(gathering(rows)[-1])
    filled = count[0]

    def note(g, ends):
        front, back = ends
        for q in range(GROUP):
            s = g * GROUP + q
            used = jnp.where(s < filled, 1, 0)
            away = coords[0, s] ^ coords[1, s]
            flag = ((away >> late) & used) ^ used
            spot = jnp.where(flag == 1, front, back - 1)
            lists[jnp.where(used == 1, spot, slots)] = s
            front, back = front + flag, back - used + flag
        return front, back

    splits[0], splits[1] = lax.fori_loop(0, slots // GROUP, note, (0, slots))


def halving(n):
    bits = [1 << i for i in reversed(range(n.bit_length() - 1))]
    return bits[1:] + bits[:1]


def partners(n, offset):
    return [(i, i ^ offset) for i in range(n)]


def body(vectors, tiles, tile_coords, tile_count):
    rows, cols = lax.axis_size("row"), lax.axis_size("col")
    repeats, vec, width = vectors.shape[0], vectors.shape[3], vectors.shape[4]
    slots = tiles.shape[2]
    if rows & (rows - 1) or cols & (cols - 1) or slots % GROUP:
        raise ValueError("sizes")
    mine = vectors.reshape(repeats, vec, width)
    mats = tiles.reshape(slots, width, width)
    coords = tile_coords.reshape(slots, 2).T
    coded_rows = repeats * vec + extra_rows(repeats)

    vmem = pl.BlockSpec(memory_space=pltpu.VMEM)
    far = pl.BlockSpec(memory_space=pl.ANY)
    anchor = pl.pallas_call(
        anchor_kernel,
        out_shape=jax.ShapeDtypeStruct((8, 128), jnp.float32),
        out_specs=vmem,
        compiler_params=pltpu.CompilerParams(vmem_limit_bytes=1 << 20),
        cost_estimate=pl.CostEstimate(flops=1 << 36, bytes_accessed=1 << 10, transcendentals=0),
        name="anchor",
    )()
    smem = pl.BlockSpec(memory_space=pltpu.SMEM)
    near = pl.pallas_call(
        prepare_kernel,
        out_shape=jax.ShapeDtypeStruct(mine.shape, mine.dtype),
        in_specs=[vmem, far],
        out_specs=vmem,
        scratch_shapes=[pltpu.SemaphoreType.DMA],
        compiler_params=pltpu.CompilerParams(vmem_limit_bytes=2 << 20),
        cost_estimate=pl.CostEstimate(flops=0, bytes_accessed=1 << 20, transcendentals=0),
        name="prepare",
    )(anchor, mine)
    filled = tile_count.reshape(1)

    pieces, offsets = [mine], [0]
    bit = cols // 2
    while bit:
        moved = []
        for piece in pieces:
            moved.append(lax.ppermute(piece, "col", partners(cols, bit)))
        pieces += moved
        offsets += [o ^ bit for o in offsets]
        bit //= 2
    pieces[0] = near
    row_pieces = [piece for _, piece in sorted(zip(offsets, pieces), key=lambda pair: pair[0])]

    column_pieces = [near]
    bit = rows // 2
    while bit:
        held = jnp.concatenate(column_pieces, axis=0) if bit < rows // 2 else mine
        column_pieces.append(lax.ppermute(held, "row", partners(rows, bit)))
        bit //= 2

    params = pltpu.CompilerParams(vmem_limit_bytes=16 << 20)
    cost = pl.CostEstimate(
        flops=slots * vec * width * width, bytes_accessed=slots * width * width, transcendentals=0
    )
    small = pl.CostEstimate(flops=0, bytes_accessed=1 << 20, transcendentals=0)

    def coded(n):
        return jax.ShapeDtypeStruct((n, coded_rows, width), jnp.int16)

    def blocks(n):
        return jax.ShapeDtypeStruct((n * repeats, vec, width), jnp.float32)

    order = halving(rows)
    held = list(range(rows))
    away = [o for o in held if o & order[0]]
    total, sent = pl.pallas_call(
        functools.partial(mirror_kernel, rows, cols, repeats, away),
        out_shape=[blocks(rows), coded(len(away))],
        in_specs=[smem, smem] + [vmem] * (1 + cols),
        out_specs=[vmem, vmem],
        scratch_shapes=[pltpu.VMEM((cols * repeats, vec, width), jnp.bfloat16)],
        compiler_params=params,
        cost_estimate=cost,
        name="mirror",
    )(filled, coords, mats, *row_pieces)

    splits, lists = pl.pallas_call(
        functools.partial(plan_kernel, rows, slots),
        out_shape=[jax.ShapeDtypeStruct((2,), jnp.int32), jax.ShapeDtypeStruct((slots + GROUP,), jnp.int32)],
        in_specs=[smem, smem, vmem],
        out_specs=[smem, smem],
        compiler_params=pltpu.CompilerParams(vmem_limit_bytes=2 << 20),
        cost_estimate=small,
        name="plan",
    )(filled, coords, near)
    plan = (splits, lists, coords)
    for step, bit in enumerate(order):
        received = lax.ppermute(sent, "row", partners(rows, bit))
        if step == len(order) - 1:
            break
        stay = [i for i, o in enumerate(held) if not o & bit]
        left = [held[i] for i in stay]
        following = order[step + 1]
        go = [i for i, o in enumerate(left) if o & following]
        total, sent = pl.pallas_call(
            functools.partial(fold_kernel, repeats, vec, stay, go),
            out_shape=[blocks(len(left) - len(go)), coded(len(go))],
            in_specs=[vmem, vmem],
            out_specs=[vmem, vmem],
            compiler_params=params,
            cost_estimate=small,
        )(total, received)
        held = [o for o in left if not o & following]

    begun = pl.pallas_call(
        functools.partial(early_kernel, rows, cols, repeats),
        out_shape=blocks(cols),
        in_specs=[smem] * 3 + [vmem] * len(column_pieces),
        out_specs=vmem,
        scratch_shapes=[pltpu.VMEM((rows // 2 * repeats, vec, width), jnp.bfloat16)],
        compiler_params=params,
        cost_estimate=cost,
        name="early",
    )(*plan, mats, *column_pieces[:-1])
    own, *partial = pl.pallas_call(
        functools.partial(forward_kernel, rows, cols, repeats),
        out_shape=[blocks(1)] + [jax.ShapeDtypeStruct((coded_rows, width), jnp.int16)] * (cols - 1),
        in_specs=[smem] * 3 + [vmem] * 3,
        out_specs=[vmem] * cols,
        scratch_shapes=[pltpu.VMEM((cols * repeats, vec, width), jnp.float32)],
        compiler_params=params,
        cost_estimate=cost,
        name="forward",
    )(*plan, mats, begun, column_pieces[-1])
    gathered = []
    for o, part in enumerate(partial):
        gathered.append(lax.ppermute(part, "col", partners(cols, o + 1)))

    out = pl.pallas_call(
        functools.partial(final_kernel, repeats),
        out_shape=blocks(1),
        in_specs=[vmem] * (2 + cols),
        out_specs=vmem,
        compiler_params=params,
        name="final",
    )(total, own, received.reshape(coded_rows, width), *gathered)
    return out.reshape(repeats, 1, 1, vec, width)


def solution(mesh):
    return jax.shard_map(
        body,
        mesh=mesh,
        in_specs=(
            P(None, "col", "row", None, None),
            P("row", "col", None, None, None),
            P("row", "col", None, None),
            P("row", "col"),
        ),
        out_specs=P(None, "col", "row", None, None),
        check_vma=False,
    )
```
